32 devices in a mesh: row: 4 (over y, core), col: 8 (over z, x).
Axes of the slice: x: 2, y: 2, z: 4, core: 2. Of those that a mesh axis runs over, the one named last changes fastest.
Arguments:
- coarse_feats: bfloat16 [8192, 512], P(('row', 'col')), may hold values from -6 to 6
- fine_feats: bfloat16 [32768, 256], P(('row', 'col')), may hold values from -6 to 6
- parent_index: int32 [32768], P(('row', 'col')), may hold values from 0 to 8191, as said below
- nbr_offset: int32 [27, 32768], P(None, ('row', 'col')), may hold values from -256 to 257, as said below
- z_position: int32 [32768], P(('row', 'col')), may hold values from 0 to 32767, as said below
- segment_id: int32 [32768], P(('row', 'col')), may hold values from 0 to 63, never falling along the last dimension, each value on 1 to 2048 neighbouring positions
- w_parent: bfloat16 [512, 256], replicated, may hold values from -0.25 to 0.25
- w_skip: bfloat16 [256, 256], replicated, may hold values from -0.375 to 0.375
- conv_taps: float32 [27, 256], replicated, may hold values from -1.5 to 1.5
- w_cpe: bfloat16 [256, 256], replicated, may hold values from -0.375 to 0.375
- w_qkv: bfloat16 [256, 768], replicated
- w_out: bfloat16 [256, 256], replicated, may hold values from -0.375 to 0.375
- w_up: bfloat16 [256, 1024], replicated, may hold values from -0.375 to 0.375
- w_down: bfloat16 [1024, 256], replicated, may hold values from -0.1875 to 0.1875
- w_cls: bfloat16 [13, 256], replicated, may hold values from -0.375 to 0.375
Outputs:
- logits: float32 [13, 32768], P(None, ('row', 'col'))
The draws below stay inside these ranges and needn't reach their ends.
Inputs may be any that keep to these rules, and one draw needn't show every extreme that they name: parent_index[g] differs from g // 4 by at most 128; it is that far below at the first point of every device's shard and that far above at the last, where the grid allows. `nbr_offset`: the offset for kernel position 13 is 0; present neighbours lie inside the grid; the first kernel offset of each shard's first point is -256 and the last offset of each shard's last point is 256, where the grid allows. `z_position`: a permutation; at most 64 of one device's 1024 points have z positions in one device's block of 1024 consecutive z positions, and exactly 64 for some pairs of devices.
All inputs are finite; a program needn't handle non-finite values.
Results may differ from the reference program's by a relative error of at most 0.014.
The reference program's roundings to bfloat16 on the way count: a program that leaves them out, or rounds other values in their place, can miss the bound.
Values may be sent and summed in bfloat16 or wider, within the bound.
A program may use at most 64 MiB of HBM per device.

```python
import math
import jax
import jax.numpy as jnp
import numpy as np
from jax import lax

D = 256
DC = 512
HEADS = 16
HID = 1024
CLASSES = 13
TAPS = 27
PATCH = 1024
FINE_DEV = 1024
COARSE_DEV = 256
REACH = 256
FINE = 32768
COARSE = 8192
HEAD_DIM = 16
DEVICES = 32


def draw_parent_index(key, part):
    points = jnp.arange(FINE, dtype=jnp.int32)
    half_span = COARSE_DEV // 2
    offsets = jax.random.randint(key, (FINE,), -half_span, half_span + 1, dtype=jnp.int32)
    local_row = points % FINE_DEV
    offsets = jnp.where(local_row == 0, -half_span, offsets)
    offsets = jnp.where(local_row == FINE_DEV - 1, half_span, offsets)
    return jnp.clip(points // 4 + offsets, 0, COARSE - 1).astype(jnp.int32)


def draw_nbr_offset(key, part):
    first_key = jax.random.fold_in(key, 11)
    second_key = jax.random.fold_in(key, 12)
    points = jnp.arange(FINE, dtype=jnp.int32)[None, :]
    tap_ids = jnp.arange(TAPS, dtype=jnp.int32)[:, None]
    offsets = jax.random.randint(first_key, (TAPS, FINE), -REACH, REACH + 1, dtype=jnp.int32)
    missing = jax.random.randint(second_key, (TAPS, FINE), 0, 3, dtype=jnp.int32) == 0
    offsets = jnp.where(missing, REACH + 1, offsets)
    offsets = jnp.where(tap_ids == TAPS // 2, 0, offsets)
    local_row = points % FINE_DEV
    offsets = jnp.where((tap_ids == 0) & (local_row == 0), -REACH, offsets)
    offsets = jnp.where((tap_ids == TAPS - 1) & (local_row == FINE_DEV - 1), REACH, offsets)
    target = points + offsets
    outside = (offsets != REACH + 1) & ((target < 0) | (target >= FINE))
    return jnp.where(outside, REACH + 1, offsets).astype(jnp.int32)


def draw_z_position(key, part):
    count = DEVICES
    share = FINE_DEV // DEVICES
    level_key = jax.random.fold_in(key, 21)
    source_key = jax.random.fold_in(key, 22)
    target_key = jax.random.fold_in(key, 23)
    levels = jnp.concatenate([jnp.full((count // 4,), 2 * share, jnp.int32), jnp.full((count // 2,), share, jnp.int32), jnp.zeros((count - count // 4 - count // 2,), jnp.int32)])
    weights = jax.random.permutation(level_key, levels)
    segment_ends = jnp.cumsum(weights)
    slot_ids = jnp.arange(FINE_DEV, dtype=jnp.int32)
    shift_of_slot = jnp.sum((slot_ids[:, None] >= segment_ends[None, :]).astype(jnp.int32), axis=1)
    device_ids = jnp.arange(count, dtype=jnp.int32)
    source_perm = jax.vmap(lambda dev_id: jax.random.permutation(jax.random.fold_in(source_key, dev_id), FINE_DEV))(device_ids).astype(jnp.int32)
    target_perm = jax.vmap(lambda dev_id: jax.random.permutation(jax.random.fold_in(target_key, dev_id), FINE_DEV))(device_ids).astype(jnp.int32)
    dest_dev = (device_ids[:, None] + shift_of_slot[None, :]) % count
    z_values = dest_dev * FINE_DEV + target_perm[dest_dev, slot_ids[None, :]]
    hilbert_rows = device_ids[:, None] * FINE_DEV + source_perm
    return jnp.zeros((FINE,), jnp.int32).at[hilbert_rows.reshape(-1)].set(z_values.reshape(-1).astype(jnp.int32))


def draw_w_qkv(key, part):
    base = jax.random.normal(key, (D, 3 * D), jnp.float32) * D ** (-0.5)
    return base.astype(jnp.bfloat16)


def shard_levels(stream_key, extent, pieces, smallest, largest):
    def one(position, blocks):
        heights = jax.random.uniform(jax.random.fold_in(jax.random.fold_in(stream_key, 6), position), (blocks,), jnp.float32, smallest / len(pieces), largest / len(pieces))
        return jnp.repeat(jnp.exp(heights), extent[position] // blocks).reshape((-1,) + (1,) * (len(extent) - position - 1))

    gain = one(*pieces[0])
    for cut in pieces[1:]:
        gain = gain * one(*cut)
    return gain


def length_profile(amount, total, limit, slope):
    loads = [(1 << 20) // math.isqrt(grade ** slope) + 1 for grade in range(2, amount + 1)]
    surplus, holding = total - limit - (amount - 1), [1] * (amount - 1)
    while surplus > 0:
        candidates = [i for i in range(amount - 1) if holding[i] < limit]
        mass, remaining = sum([loads[i] for i in candidates]), surplus
        for i in candidates:
            addition = min(limit - holding[i], max(1, remaining * loads[i] // mass), surplus)
            holding[i] = holding[i] + addition
            surplus = surplus - addition
    return np.array([limit] + holding)


def ragged_sizes(key, number_of, total, reach, lean):
    if number_of == 2:
        one = jax.random.randint(key, (), max(1, total - reach), min(reach, total - 1) + 1)
        return jnp.stack([one, total - one])
    sizes = jnp.asarray(length_profile(number_of, total, reach, lean), jnp.int32)
    twos = (number_of - 1) // 2
    source_of, receiver = sizes[1:1 + 2 * twos:2], sizes[2:2 + 2 * twos:2]
    slack = jnp.minimum(source_of - 1, reach - receiver)
    moved = jax.random.randint(jax.random.fold_in(key, 1), (twos,), 0, 1 << 20) % (slack + 1)
    sizes = sizes.at[1:1 + 2 * twos:2].set(source_of - moved).at[2:2 + 2 * twos:2].set(receiver + moved)
    return sizes[jax.random.permutation(jax.random.fold_in(key, 2), number_of)]


def bell_draw(rng, extent, scale, reach, shards=(), held_as=jnp.bfloat16):
    entries = jax.random.normal(rng, extent, jnp.float32) * scale
    if len(shards) > 0:
        entries = shard_levels(rng, extent, shards, -0.22, 0.18) * entries
    return jnp.clip(entries, min=-reach, max=reach).astype(held_as)


def setup_inputs(seed: int = 0) -> dict:
    arg_keys = jax.random.split(jax.random.key(seed), 16)
    coarse_feats = bell_draw(arg_keys[0], (COARSE, DC), 1.0, 6.0, ((0, 32),))
    fine_feats = bell_draw(arg_keys[1], (FINE, D), 1.0, 6.0, ((0, 32),))
    parent_index = draw_parent_index(jax.random.fold_in(arg_keys[15], 71), 0)
    nbr_offset = draw_nbr_offset(jax.random.fold_in(arg_keys[15], 71), 0)
    z_position = draw_z_position(jax.random.fold_in(arg_keys[15], 71), 0)
    segment_id = jnp.searchsorted(jnp.cumsum(ragged_sizes(arg_keys[5], FINE // 512, FINE, 2048, 2)), jnp.arange(FINE), side="right").astype(jnp.int32)
    w_parent = bell_draw(arg_keys[6], (DC, D), DC ** -0.5, 0.25)
    w_skip = bell_draw(arg_keys[7], (D, D), D ** -0.5, 0.375)
    conv_taps = bell_draw(arg_keys[8], (TAPS, D), 0.25, 1.5, (), jnp.float32)
    w_cpe = bell_draw(arg_keys[9], (D, D), D ** -0.5, 0.375)
    w_qkv = draw_w_qkv(jax.random.fold_in(arg_keys[15], 71), 0)
    w_out = bell_draw(arg_keys[11], (D, D), D ** -0.5, 0.375)
    w_up = bell_draw(arg_keys[12], (D, HID), D ** -0.5, 0.375)
    w_down = bell_draw(arg_keys[13], (HID, D), HID ** -0.5, 0.1875)
    w_cls = bell_draw(arg_keys[14], (CLASSES, D), D ** -0.5, 0.375)
    return {"coarse_feats": coarse_feats, "fine_feats": fine_feats, "parent_index": parent_index, "nbr_offset": nbr_offset, "z_position": z_position, "segment_id": segment_id, "w_parent": w_parent, "w_skip": w_skip, "conv_taps": conv_taps, "w_cpe": w_cpe, "w_qkv": w_qkv, "w_out": w_out, "w_up": w_up, "w_down": w_down, "w_cls": w_cls}


def layer_norm(values):
    center = values - lax.optimization_barrier(jnp.mean(values, axis=-1, keepdims=True))
    spread = lax.optimization_barrier(jnp.mean(center * center, axis=-1, keepdims=True))
    return center * lax.rsqrt(spread + 1e-05)

def attend_all(z_feats, segment_id, w_qkv, w_out):
    normed = layer_norm(z_feats.astype(jnp.float32)).astype(jnp.bfloat16)
    qkv_all = jnp.dot(normed, w_qkv, preferred_element_type=jnp.float32).astype(jnp.bfloat16)
    scale_factor = HEAD_DIM ** (-0.5)

    def one_patch(start):
        block = lax.dynamic_slice_in_dim(qkv_all, start, PATCH, 0).astype(jnp.float32)
        seg_block = lax.dynamic_slice_in_dim(segment_id, start, PATCH, 0)
        same_seg = seg_block[:, None] == seg_block[None, :]
        split = block.reshape(PATCH, 3, HEADS, HEAD_DIM)
        scores = jnp.einsum('qhd,khd->hqk', split[:, 0], split[:, 1]) * scale_factor
        scores = jnp.where(same_seg[None], scores, -1e+30)
        row_max = lax.optimization_barrier(jnp.max(scores, axis=-1, keepdims=True))
        exp_scores = jnp.exp(scores - row_max)
        probs = (exp_scores / lax.optimization_barrier(jnp.sum(exp_scores, axis=-1, keepdims=True))).astype(jnp.bfloat16)
        out_heads = jnp.einsum('hqk,khd->qhd', probs.astype(jnp.float32), split[:, 2])
        return out_heads.reshape(PATCH, D).astype(jnp.bfloat16)
    starts = (jnp.arange(FINE // PATCH) * PATCH).astype(jnp.int32)
    att = lax.map(one_patch, starts).reshape(FINE, D)
    return jnp.dot(att, w_out, preferred_element_type=jnp.float32).astype(jnp.bfloat16)

def reference(coarse_feats, fine_feats, parent_index, nbr_offset, z_position, segment_id, w_parent, w_skip, conv_taps, w_cpe, w_qkv, w_out, w_up, w_down, w_cls):
    parent = jax.nn.gelu(layer_norm(jnp.dot(coarse_feats, w_parent, preferred_element_type=jnp.float32))).astype(jnp.bfloat16)
    skip = jax.nn.gelu(layer_norm(jnp.dot(fine_feats, w_skip, preferred_element_type=jnp.float32)))
    feat = (parent[parent_index].astype(jnp.float32) + skip).astype(jnp.bfloat16)
    point_index = jnp.arange(FINE, dtype=jnp.int32)

    def add_tap(tap_index, running):
        offsets = nbr_offset[tap_index]
        present = offsets != REACH + 1
        source = jnp.where(present, point_index + offsets, 0).astype(jnp.int32)
        gathered = feat[source].astype(jnp.float32) * conv_taps[tap_index][None, :]
        return running + jnp.where(present[:, None], gathered, jnp.float32(0.0))
    conv = lax.fori_loop(0, TAPS, add_tap, jnp.zeros((FINE, D), jnp.float32)).astype(jnp.bfloat16)
    x_feats = (feat.astype(jnp.float32) + layer_norm(jnp.dot(conv, w_cpe, preferred_element_type=jnp.float32))).astype(jnp.bfloat16)
    z_feats = jnp.zeros_like(x_feats).at[z_position].set(x_feats)
    att_out = attend_all(z_feats, segment_id, w_qkv, w_out)
    x_two = x_feats.astype(jnp.float32) + att_out[z_position].astype(jnp.float32)
    hidden = jax.nn.gelu(jnp.dot(layer_norm(x_two).astype(jnp.bfloat16), w_up, preferred_element_type=jnp.float32)).astype(jnp.bfloat16)
    x_three = x_two + jnp.dot(hidden, w_down, preferred_element_type=jnp.float32)
    final_norm = layer_norm(x_three).astype(jnp.bfloat16)
    return jnp.dot(w_cls, final_norm.T, preferred_element_type=jnp.float32)
```

```python
import functools

import jax
import jax.numpy as jnp
from jax import lax
from jax.experimental import pallas as pl
from jax.experimental.pallas import tpu as pltpu
from jax.sharding import PartitionSpec as P

HEADS = 16
PATCH = 1024
REACH = 256
AXES = ("row", "col")
BF = jnp.bfloat16
F32 = jnp.float32
I32 = jnp.int32
VM = pl.BlockSpec(memory_space=pltpu.VMEM)


def dot(a, b):
    return jnp.dot(a, b, preferred_element_type=F32)


def dot_nt(a, b):
    return lax.dot_general(a, b, (((1,), (1,)), ((), ())), preferred_element_type=F32)


def layer_norm(values):
    center = values - jnp.mean(values, axis=-1, keepdims=True)
    spread = jnp.mean(center * center, axis=-1, keepdims=True)
    return center * lax.rsqrt(spread + 1e-05)


def pick(index, rows, cols, dim):
    grid = lax.broadcasted_iota(I32, (rows, cols), dim)
    return jnp.where(grid == index, 1.0, 0.0).astype(BF)


def halo(cells, width, dim):
    count = lax.axis_size(AXES)
    head = lax.slice_in_dim(cells, 0, width, axis=dim)
    tail = lax.slice_in_dim(cells, cells.shape[dim] - width, cells.shape[dim], axis=dim)
    low = lax.ppermute(tail, AXES, [(i, i + 1) for i in range(count - 1)])
    high = lax.ppermute(head, AXES, [(i + 1, i) for i in range(count - 1)])
    return jnp.concatenate([low, cells, high], axis=dim)


def rank_kernel(devices, capacity, z_ref, pos_ref, slot_ref):
    rows = z_ref.shape[1]
    z = z_ref[...]
    dest = z // rows
    slot = z % rows
    onehot = pick(dest, devices, rows, 0)
    before = lax.broadcasted_iota(I32, (rows, rows), 0) < lax.broadcasted_iota(I32, (rows, rows), 1)
    ahead = dot(onehot, jnp.where(before, 1.0, 0.0).astype(BF))
    rank = jnp.sum(ahead * onehot.astype(F32), axis=0, keepdims=True).astype(I32)
    pos = dest * capacity + rank
    pos_ref[...] = pos
    code = slot + 1
    part = lax.broadcasted_iota(I32, (16, rows), 0)
    digits = jnp.where(part == 0, code // 32, jnp.where(part == 1, code % 32, 0))
    digits = digits.astype(F32).astype(BF)
    total = devices * capacity
    step = min(512, total)
    for start in range(0, total, step):
        got = dot_nt(digits, pick(pos - start, step, rows, 0)).astype(I32)
        slot_ref[:, start : start + step] = got[0:1] * 32 + got[1:2] - 1


def conv_kernel(
    coarse_ref, fine_ref, parent_ref, nbr_ref, pos_ref,
    w_parent_ref, w_skip_ref, taps_ref, w_cpe_ref,
    x_ref, send_ref, feat_ref, par_ref,
):
    rows = x_ref.shape[0]
    ext = fine_ref.shape[0]
    coarse = coarse_ref.shape[0]
    par_ref[...] = jax.nn.gelu(layer_norm(dot(coarse_ref[...], w_parent_ref[...]))).astype(BF)
    block = 256

    def join(i, carry):
        at = pl.ds(pl.multiple_of(i * block, block), block)
        chosen = dot(pick(parent_ref[at, :], block, coarse, 1), par_ref[...])
        skip = jax.nn.gelu(layer_norm(dot(fine_ref[at, :], w_skip_ref[...])))
        feat_ref[at, :] = (chosen + skip).astype(BF)
        return carry

    lax.fori_loop(0, ext // block, join, 0)
    window = block + 2 * REACH

    def conv(i, carry):
        base = pl.multiple_of(i * block, block)
        at = pl.ds(base, block)
        cells = feat_ref[pl.ds(base, window), :]
        offsets = nbr_ref[at, :]
        here = lax.broadcasted_iota(I32, offsets.shape, 0) + REACH
        source = jnp.where(offsets != REACH + 1, here + offsets, -1)
        total = jnp.zeros((block, cells.shape[1]), F32)
        for t in range(nbr_ref.shape[1]):
            total = total + dot(pick(source[:, t : t + 1], block, window, 1), cells) * taps_ref[t : t + 1, :]
        out = layer_norm(dot(total.astype(BF), w_cpe_ref[...]))
        center = feat_ref[pl.ds(base + REACH, block), :]
        x_ref[at, :] = (center.astype(F32) + out).astype(BF)
        return carry

    lax.fori_loop(0, rows // block, conv, 0)
    pos = pos_ref[...]

    def pack(i, carry):
        at = pl.ds(pl.multiple_of(i * block, block), block)
        send_ref[at, :] = dot(pick(pos - i * block, block, rows, 0), x_ref[...]).astype(BF)
        return carry

    lax.fori_loop(0, send_ref.shape[0] // block, pack, 0)


def attend_kernel(
    recv_ref, slot_row_ref, slot_col_ref, seg_ref, w_qkv_ref,
    back_ref, q_ref, k_ref, v_ref, fq_ref, fk_ref, acc_ref,
):
    rows, width = acc_ref.shape
    total = recv_ref.shape[0]
    head_dim = width // HEADS
    lanes = 128
    per_group = lanes // head_dim
    block = 256

    def unpack(i, carry):
        at = pl.ds(pl.multiple_of(i * block, block), block)
        z = dot(pick(slot_row_ref[...] - i * block, block, total, 0), recv_ref[...])
        normed = layer_norm(z).astype(BF)
        qkv = dot(normed, w_qkv_ref[...])
        q_ref[at, :] = qkv[:, :width].astype(BF) * jnp.asarray(head_dim**-0.5, BF)
        k_ref[at, :] = qkv[:, width : 2 * width].astype(BF)
        v_ref[at, :] = qkv[:, 2 * width :].astype(BF)
        return carry

    lax.fori_loop(0, rows // block, unpack, 0)
    bits = (PATCH - 1).bit_length()
    lane = lax.broadcasted_iota(I32, (rows, lanes), 1)
    seg = jnp.broadcast_to(seg_ref[...] - seg_ref[0:1, :], (rows, lanes))
    code = ((seg >> (lane // 2)) & 1) ^ (lane & 1)
    used = lane < 2 * bits
    fq_ref[...] = jnp.where(used & (code == 1), 1.0, 0.0).astype(BF)
    fk_ref[...] = jnp.where(used & (code == 0), -1e30, 0.0).astype(BF)
    acc_ref[...] = jnp.zeros_like(acc_ref)
    owner = lane // head_dim

    for g in range(width // lanes):
        cols = slice(g * lanes, (g + 1) * lanes)

        def head(h, carry):
            mine = owner == h
            keys = jnp.where(mine, k_ref[:, cols], jnp.zeros((), BF))
            keys = jnp.concatenate([keys, fk_ref[...]], axis=1)
            values = jnp.where(mine, v_ref[:, cols], jnp.zeros((), BF))
            values = jnp.concatenate([values, jnp.ones((rows, lanes), BF)], axis=1)
            for start in range(0, rows, block):
                at = slice(start, start + block)
                query = jnp.concatenate([q_ref[at, cols], fq_ref[at, :]], axis=1)
                scores = dot_nt(query, keys)
                top = jnp.max(scores, axis=-1, keepdims=True)
                probs = jnp.exp(scores - top).astype(BF)
                out = dot(probs, values)
                acc_ref[at, cols] += out[:, :lanes] / out[:, lanes:]
            return carry

        lax.fori_loop(0, per_group, head, 0)

    q_ref[...] = acc_ref[...].astype(BF)

    def pack(i, carry):
        at = pl.ds(pl.multiple_of(i * block, block), block)
        back_ref[at, :] = dot(pick(slot_col_ref[at, :], block, rows, 1), q_ref[...]).astype(BF)
        return carry

    lax.fori_loop(0, total // block, pack, 0)


def head_kernel(x_ref, back_ref, pos_ref, w_out_ref, w_up_ref, w_down_ref, w_cls_ref, out_ref):
    rows = x_ref.shape[0]
    total = back_ref.shape[0]
    block = 256
    for start in range(0, rows, block):
        at = slice(start, start + block)
        home = dot(pick(pos_ref[at, :], block, total, 1), back_ref[...]).astype(BF)
        o = dot(home, w_out_ref[...]).astype(BF)
        x_two = x_ref[at, :].astype(F32) + o.astype(F32)
        hidden = jax.nn.gelu(dot(layer_norm(x_two).astype(BF), w_up_ref[...])).astype(BF)
        x_three = x_two + dot(hidden, w_down_ref[...])
        out_ref[:, at] = dot_nt(w_cls_ref[...], layer_norm(x_three).astype(BF))


def local(
    coarse_feats,
    fine_feats,
    parent_index,
    nbr_offset,
    z_position,
    segment_id,
    w_parent,
    w_skip,
    conv_taps,
    w_cpe,
    w_qkv,
    w_out,
    w_up,
    w_down,
    w_cls,
):
    fine_rows, width = fine_feats.shape
    coarse_rows = coarse_feats.shape[0]
    devices = lax.axis_size(AXES)
    dev_index = lax.axis_index(AXES)
    capacity = 2 * fine_rows // devices
    total = devices * capacity
    assert fine_rows == PATCH

    pos, slots = pl.pallas_call(
        functools.partial(rank_kernel, devices, capacity),
        out_shape=(
            jax.ShapeDtypeStruct((1, fine_rows), I32),
            jax.ShapeDtypeStruct((1, total), I32),
        ),
        in_specs=[VM],
        out_specs=(VM, VM),
    )(z_position.reshape(1, fine_rows))
    recv_slots = lax.all_to_all(
        slots.reshape(devices, capacity), AXES, split_axis=0, concat_axis=0, tiled=True
    )

    fine_per_coarse = fine_rows // coarse_rows
    margin = coarse_rows // 2 + REACH // fine_per_coarse
    coarse_ext = halo(coarse_feats, margin, 0)
    fine_ext = halo(fine_feats, REACH, 0)
    parent_ext = halo(parent_index, REACH, 0) - (dev_index * coarse_rows - margin)
    ext = fine_rows + 2 * REACH
    x_feats, send = pl.pallas_call(
        conv_kernel,
        out_shape=(
            jax.ShapeDtypeStruct((fine_rows, width), BF),
            jax.ShapeDtypeStruct((total, width), BF),
        ),
        in_specs=[VM] * 9,
        out_specs=(VM, VM),
        scratch_shapes=[
            pltpu.VMEM((ext, width), BF),
            pltpu.VMEM((coarse_ext.shape[0], width), BF),
        ],
    )(
        coarse_ext, fine_ext, parent_ext.reshape(ext, 1), nbr_offset.T, pos,
        w_parent, w_skip, conv_taps, w_cpe,
    )
    recv = lax.all_to_all(
        send.reshape(devices, capacity, width), AXES, split_axis=0, concat_axis=0, tiled=True
    ).reshape(total, width)

    back = pl.pallas_call(
        attend_kernel,
        out_shape=jax.ShapeDtypeStruct((total, width), BF),
        in_specs=[VM] * 5,
        out_specs=VM,
        scratch_shapes=[
            pltpu.VMEM((fine_rows, width), BF),
            pltpu.VMEM((fine_rows, width), BF),
            pltpu.VMEM((fine_rows, width), BF),
            pltpu.VMEM((fine_rows, 128), BF),
            pltpu.VMEM((fine_rows, 128), BF),
            pltpu.VMEM((fine_rows, width), F32),
        ],
    )(
        recv, recv_slots.reshape(1, total), recv_slots.reshape(total, 1),
        segment_id.reshape(fine_rows, 1), w_qkv,
    )
    returned = lax.all_to_all(
        back.reshape(devices, capacity, width), AXES, split_axis=0, concat_axis=0, tiled=True
    ).reshape(total, width)
    return pl.pallas_call(
        head_kernel,
        out_shape=jax.ShapeDtypeStruct((w_cls.shape[0], fine_rows), F32),
        in_specs=[VM] * 7,
        out_specs=VM,
    )(x_feats, returned, pos.reshape(fine_rows, 1), w_out, w_up, w_down, w_cls)


def solution(mesh):
    rows = P(AXES, None)
    flat = P(AXES)
    placed = (rows, rows, flat, P(None, AXES), flat, flat) + (P(),) * 9
    return jax.shard_map(
        local, mesh=mesh, in_specs=placed, out_specs=P(None, AXES), check_vma=False
    )
```

```python
import functools

import jax
import jax.numpy as jnp
from jax import lax
from jax.experimental import pallas as pl
from jax.experimental.pallas import tpu as pltpu
from jax.sharding import PartitionSpec as P

HEADS = 16
PATCH = 1024
REACH = 256
AXES = ("row", "col")
BF = jnp.bfloat16
F32 = jnp.float32
I32 = jnp.int32
VM = pl.BlockSpec(memory_space=pltpu.VMEM)


def dot(a, b):
    return jnp.dot(a, b, preferred_element_type=F32)


def dot_nt(a, b):
    return lax.dot_general(a, b, (((1,), (1,)), ((), ())), preferred_element_type=F32)


def layer_norm(values):
    center = values - jnp.mean(values, axis=-1, keepdims=True)
    spread = jnp.mean(center * center, axis=-1, keepdims=True)
    return center * lax.rsqrt(spread + 1e-05)


def pick(index, rows, cols, dim):
    grid = lax.broadcasted_iota(I32, (rows, cols), dim)
    return jnp.where(grid == index, 1.0, 0.0).astype(BF)


def column(row):
    return jnp.broadcast_to(row, (128, row.shape[1])).T[:, :1]


def place(device):
    inner = lax.axis_size("col")
    return (device // inner, device % inner)


def greet(me, devices):
    barrier = pltpu.get_barrier_semaphore()

    def signal(k, carry):
        pl.semaphore_signal(
            barrier, inc=1, device_id=place((me + k) % devices),
            device_id_type=pl.DeviceIdType.MESH,
        )
        return carry

    lax.fori_loop(1, devices, signal, 0)
    pl.semaphore_wait(barrier, devices - 1)


def ship(src, dst, send_sem, recv_sem, device):
    return pltpu.make_async_remote_copy(
        src_ref=src, dst_ref=dst, send_sem=send_sem, recv_sem=recv_sem,
        device_id=place(device), device_id_type=pl.DeviceIdType.MESH,
    )


def spread(src_ref, dst_ref, send_sems, recv_sems, me, devices):
    def start(k, carry):
        peer = (me + k) % devices
        ship(
            src_ref.at[peer], dst_ref.at[me], send_sems.at[peer], recv_sems.at[me], peer
        ).start()
        return carry

    lax.fori_loop(1, devices, start, 0)


def gather_in(src_ref, dst_ref, send_sems, recv_sems, me, devices):
    def finish(k, carry):
        peer = (me + k) % devices
        ship(
            src_ref.at[peer], dst_ref.at[peer], send_sems.at[peer], recv_sems.at[peer], peer
        ).wait()
        return carry

    lax.fori_loop(1, devices, finish, 0)


def trade_kernel(devices, src_ref, dst_ref, send_sems, recv_sems):
    me = lax.axis_index(AXES)
    greet(me, devices)
    spread(src_ref, dst_ref, send_sems, recv_sems, me, devices)
    dst_ref[me] = src_ref[me]
    gather_in(src_ref, dst_ref, send_sems, recv_sems, me, devices)


def trade(cells, collective_id):
    devices = cells.shape[0]
    return pl.pallas_call(
        functools.partial(trade_kernel, devices),
        out_shape=jax.ShapeDtypeStruct(cells.shape, cells.dtype),
        in_specs=[VM],
        out_specs=VM,
        scratch_shapes=[
            pltpu.SemaphoreType.DMA((devices,)),
            pltpu.SemaphoreType.DMA((devices,)),
        ],
        compiler_params=pltpu.CompilerParams(
            collective_id=collective_id, has_side_effects=True
        ),
    )(cells)


def open_kernel(
    devices, capacity, z_ref, coarse_ref, fine_ref, parent_ref,
    pos_ref, got_ref, coarse_out, fine_out, parent_out,
    slot_ref, take_ref, send_sems, recv_sems, send_side, recv_side,
):
    me = lax.axis_index(AXES)
    greet(me, devices)
    after, before = (me + 1) % devices, (me + devices - 1) % devices
    moves = []
    for j, (src, dst, dim) in enumerate(
        ((coarse_ref, coarse_out, 0), (fine_ref, fine_out, 0), (parent_ref, parent_out, 1))
    ):
        size = src.shape[dim]
        width = (dst.shape[dim] - size) // 2

        def cut(ref, at, count, dim=dim):
            return ref.at[pl.ds(at, count), :] if dim == 0 else ref.at[:, pl.ds(at, count)]

        moves.append(ship(
            cut(src, size - width, width), cut(dst, 0, width),
            send_side.at[2 * j], recv_side.at[2 * j], after,
        ))
        moves.append(ship(
            cut(src, 0, width), cut(dst, size + width, width),
            send_side.at[2 * j + 1], recv_side.at[2 * j + 1], before,
        ))
    for move in moves:
        move.start()

    rows = z_ref.shape[1]
    z = z_ref[...]
    dest = z // rows
    slot = z % rows
    onehot = pick(dest, devices, rows, 0)
    earlier = lax.broadcasted_iota(I32, (rows, rows), 0) < lax.broadcasted_iota(I32, (rows, rows), 1)
    ahead = dot(onehot, jnp.where(earlier, 1.0, 0.0).astype(BF))
    rank = jnp.sum(ahead * onehot.astype(F32), axis=0, keepdims=True).astype(I32)
    pos = dest * capacity + rank
    pos_ref[...] = pos
    code = slot + 1
    part = lax.broadcasted_iota(I32, (16, rows), 0)
    digits = jnp.where(part == 0, code // 32, jnp.where(part == 1, code % 32, 0))
    digits = digits.astype(F32).astype(BF)
    total = devices * capacity
    step = min(512, total)
    for start in range(0, total, step):
        got = dot_nt(digits, pick(pos - start, step, rows, 0)).astype(I32)
        got = got[0:1] * 32 + got[1:2] - 1
        for d in range(step // capacity):
            slot_ref[start // capacity + d] = got[:, d * capacity : (d + 1) * capacity]

    spread(slot_ref, take_ref, send_sems, recv_sems, me, devices)
    take_ref[me] = slot_ref[me]
    for src, dst, dim in (
        (coarse_ref, coarse_out, 0), (fine_ref, fine_out, 0), (parent_ref, parent_out, 1)
    ):
        size = src.shape[dim]
        width = (dst.shape[dim] - size) // 2
        if dim == 0:
            dst[width : width + size, :] = src[...]
        else:
            dst[:, width : width + size] = src[...]
    for move in moves:
        move.wait()
    gather_in(slot_ref, take_ref, send_sems, recv_sems, me, devices)
    for d in range(devices):
        got_ref[:, d * capacity : (d + 1) * capacity] = take_ref[d]


def conv_kernel(
    margin, coarse_ref, fine_ref, parent_ref, nbr_ref, pos_ref,
    w_parent_ref, w_skip_ref, taps_ref, w_cpe_ref,
    x_ref, send_ref, feat_ref, par_ref,
):
    rows = x_ref.shape[0]
    ext = fine_ref.shape[0]
    coarse = coarse_ref.shape[0]
    par_ref[...] = jax.nn.gelu(layer_norm(dot(coarse_ref[...], w_parent_ref[...]))).astype(BF)
    block = 256
    base_row = lax.axis_index(AXES) * (coarse - 2 * margin) - margin

    def join(i, carry):
        at = pl.ds(pl.multiple_of(i * block, block), block)
        rows_at = column(parent_ref[:, at] - base_row)
        chosen = dot(pick(rows_at, block, coarse, 1), par_ref[...])
        skip = jax.nn.gelu(layer_norm(dot(fine_ref[at, :], w_skip_ref[...])))
        feat_ref[at, :] = (chosen + skip).astype(BF)
        return carry

    lax.fori_loop(0, ext // block, join, 0)
    window = block + 2 * REACH

    def conv(i, carry):
        base = pl.multiple_of(i * block, block)
        at = pl.ds(base, block)
        cells = feat_ref[pl.ds(base, window), :]
        offsets = nbr_ref[:, at].T
        here = lax.broadcasted_iota(I32, offsets.shape, 0) + REACH
        source = jnp.where(offsets != REACH + 1, here + offsets, -1)
        total = jnp.zeros((block, cells.shape[1]), F32)
        for t in range(nbr_ref.shape[0]):
            total = total + dot(pick(source[:, t : t + 1], block, window, 1), cells) * taps_ref[t : t + 1, :]
        out = layer_norm(dot(total.astype(BF), w_cpe_ref[...]))
        center = feat_ref[pl.ds(base + REACH, block), :]
        x_ref[at, :] = (center.astype(F32) + out).astype(BF)
        return carry

    lax.fori_loop(0, rows // block, conv, 0)
    pos = pos_ref[...]

    def pack(i, carry):
        at = pl.ds(pl.multiple_of(i * block, block), block)
        send_ref[at, :] = dot(pick(pos - i * block, block, rows, 0), x_ref[...]).astype(BF)
        return carry

    lax.fori_loop(0, send_ref.shape[0] // block, pack, 0)


def attend_kernel(
    recv_ref, slot_row_ref, seg_ref, w_qkv_ref,
    back_ref, q_ref, k_ref, v_ref, fq_ref, fk_ref, acc_ref,
):
    rows, width = acc_ref.shape
    total = recv_ref.shape[0]
    head_dim = width // HEADS
    lanes = 128
    per_group = lanes // head_dim
    block = 256

    def unpack(i, carry):
        at = pl.ds(pl.multiple_of(i * block, block), block)
        z = dot(pick(slot_row_ref[...] - i * block, block, total, 0), recv_ref[...])
        normed = layer_norm(z).astype(BF)
        qkv = dot(normed, w_qkv_ref[...])
        q_ref[at, :] = qkv[:, :width].astype(BF) * jnp.asarray(head_dim**-0.5, BF)
        k_ref[at, :] = qkv[:, width : 2 * width].astype(BF)
        v_ref[at, :] = qkv[:, 2 * width :].astype(BF)
        return carry

    lax.fori_loop(0, rows // block, unpack, 0)
    bits = (PATCH - 1).bit_length()
    lane = lax.broadcasted_iota(I32, (rows, lanes), 1)
    seg = jnp.broadcast_to(seg_ref[...] - seg_ref[:, 0:1], (lanes, rows)).T
    code = ((seg >> (lane // 2)) & 1) ^ (lane & 1)
    used = lane < 2 * bits
    fq_ref[...] = jnp.where(used & (code == 1), 1.0, 0.0).astype(BF)
    fk_ref[...] = jnp.where(used & (code == 0), -1e30, 0.0).astype(BF)
    acc_ref[...] = jnp.zeros_like(acc_ref)
    owner = lane // head_dim

    for g in range(width // lanes):
        cols = slice(g * lanes, (g + 1) * lanes)

        def head(h, carry):
            mine = owner == h
            keys = jnp.where(mine, k_ref[:, cols], jnp.zeros((), BF))
            keys = jnp.concatenate([keys, fk_ref[...]], axis=1)
            values = jnp.where(mine, v_ref[:, cols], jnp.zeros((), BF))
            values = jnp.concatenate([values, jnp.ones((rows, lanes), BF)], axis=1)
            for start in range(0, rows, block):
                at = slice(start, start + block)
                query = jnp.concatenate([q_ref[at, cols], fq_ref[at, :]], axis=1)
                scores = dot_nt(query, keys)
                top = jnp.max(scores, axis=-1, keepdims=True)
                probs = jnp.exp(scores - top).astype(BF)
                out = dot(probs, values)
                acc_ref[at, cols] += out[:, :lanes] / out[:, lanes:]
            return carry

        lax.fori_loop(0, per_group, head, 0)

    q_ref[...] = acc_ref[...].astype(BF)

    def pack(i, carry):
        at = pl.ds(pl.multiple_of(i * block, block), block)
        back_ref[at, :] = dot(pick(column(slot_row_ref[:, at]), block, rows, 1), q_ref[...]).astype(BF)
        return carry

    lax.fori_loop(0, total // block, pack, 0)


def head_kernel(x_ref, back_ref, pos_ref, w_out_ref, w_up_ref, w_down_ref, w_cls_ref, out_ref):
    rows = x_ref.shape[0]
    total = back_ref.shape[0]
    block = 256
    for start in range(0, rows, block):
        at = slice(start, start + block)
        home = dot(pick(column(pos_ref[:, at]), block, total, 1), back_ref[...]).astype(BF)
        o = dot(home, w_out_ref[...]).astype(BF)
        x_two = x_ref[at, :].astype(F32) + o.astype(F32)
        hidden = jax.nn.gelu(dot(layer_norm(x_two).astype(BF), w_up_ref[...])).astype(BF)
        x_three = x_two + dot(hidden, w_down_ref[...])
        out_ref[:, at] = dot_nt(w_cls_ref[...], layer_norm(x_three).astype(BF))


def local(
    coarse_feats,
    fine_feats,
    parent_index,
    nbr_offset,
    z_position,
    segment_id,
    w_parent,
    w_skip,
    conv_taps,
    w_cpe,
    w_qkv,
    w_out,
    w_up,
    w_down,
    w_cls,
):
    fine_rows, width = fine_feats.shape
    coarse_rows = coarse_feats.shape[0]
    devices = lax.axis_size(AXES)
    capacity = 2 * fine_rows // devices
    total = devices * capacity
    assert fine_rows == PATCH

    fine_per_coarse = fine_rows // coarse_rows
    margin = coarse_rows // 2 + REACH // fine_per_coarse
    ext = fine_rows + 2 * REACH
    coarse_ext_rows = coarse_rows + 2 * margin
    pos, slots, coarse_ext, fine_ext, parent_ext = pl.pallas_call(
        functools.partial(open_kernel, devices, capacity),
        out_shape=(
            jax.ShapeDtypeStruct((1, fine_rows), I32),
            jax.ShapeDtypeStruct((1, total), I32),
            jax.ShapeDtypeStruct((coarse_ext_rows, coarse_feats.shape[1]), BF),
            jax.ShapeDtypeStruct((ext, width), BF),
            jax.ShapeDtypeStruct((1, ext), I32),
        ),
        in_specs=[VM] * 4,
        out_specs=(VM,) * 5,
        scratch_shapes=[
            pltpu.VMEM((devices, 1, capacity), I32),
            pltpu.VMEM((devices, 1, capacity), I32),
            pltpu.SemaphoreType.DMA((devices,)),
            pltpu.SemaphoreType.DMA((devices,)),
            pltpu.SemaphoreType.DMA((6,)),
            pltpu.SemaphoreType.DMA((6,)),
        ],
        compiler_params=pltpu.CompilerParams(collective_id=0, has_side_effects=True),
    )(
        z_position.reshape(1, fine_rows), coarse_feats, fine_feats,
        parent_index.reshape(1, fine_rows),
    )
    x_feats, send = pl.pallas_call(
        functools.partial(conv_kernel, margin),
        out_shape=(
            jax.ShapeDtypeStruct((fine_rows, width), BF),
            jax.ShapeDtypeStruct((total, width), BF),
        ),
        in_specs=[VM] * 9,
        out_specs=(VM, VM),
        scratch_shapes=[
            pltpu.VMEM((ext, width), BF),
            pltpu.VMEM((coarse_ext_rows, width), BF),
        ],
    )(
        coarse_ext, fine_ext, parent_ext, nbr_offset, pos,
        w_parent, w_skip, conv_taps, w_cpe,
    )
    recv = trade(send.reshape(devices, capacity, width), 1).reshape(total, width)

    back = pl.pallas_call(
        attend_kernel,
        out_shape=jax.ShapeDtypeStruct((total, width), BF),
        in_specs=[VM] * 4,
        out_specs=VM,
        scratch_shapes=[
            pltpu.VMEM((fine_rows, width), BF),
            pltpu.VMEM((fine_rows, width), BF),
            pltpu.VMEM((fine_rows, width), BF),
            pltpu.VMEM((fine_rows, 128), BF),
            pltpu.VMEM((fine_rows, 128), BF),
            pltpu.VMEM((fine_rows, width), F32),
        ],
    )(recv, slots, segment_id.reshape(1, fine_rows), w_qkv)
    returned = trade(back.reshape(devices, capacity, width), 2).reshape(total, width)
    return pl.pallas_call(
        head_kernel,
        out_shape=jax.ShapeDtypeStruct((w_cls.shape[0], fine_rows), F32),
        in_specs=[VM] * 7,
        out_specs=VM,
    )(x_feats, returned, pos, w_out, w_up, w_down, w_cls)


def solution(mesh):
    rows = P(AXES, None)
    flat = P(AXES)
    placed = (rows, rows, flat, P(None, AXES), flat, flat) + (P(),) * 9
    return jax.shard_map(
        local, mesh=mesh, in_specs=placed, out_specs=P(None, AXES), check_vma=False
    )
```

```python
import functools

import jax
import jax.numpy as jnp
from jax import lax
from jax.experimental import pallas as pl
from jax.experimental.pallas import tpu as pltpu
from jax.sharding import PartitionSpec as P

HEADS = 16
PATCH = 1024
REACH = 256
QUERY_BLOCK = 256
AXES = ("row", "col")
BF = jnp.bfloat16
F32 = jnp.float32
I32 = jnp.int32
VM = pl.BlockSpec(memory_space=pltpu.VMEM)


def dot(a, b):
    return jnp.dot(a, b, preferred_element_type=F32)


def dot_nt(a, b):
    return lax.dot_general(a, b, (((1,), (1,)), ((), ())), preferred_element_type=F32)


def layer_norm(values):
    center = values - jnp.mean(values, axis=-1, keepdims=True)
    spread = jnp.mean(center * center, axis=-1, keepdims=True)
    return center * lax.rsqrt(spread + 1e-05)


def pick(index, rows, cols, dim):
    grid = lax.broadcasted_iota(I32, (rows, cols), dim)
    return jnp.where(grid == index, 1.0, 0.0).astype(BF)


def column(row):
    return jnp.broadcast_to(row, (128, row.shape[1])).T[:, :1]


def place(device):
    inner = lax.axis_size("col")
    return (device // inner, device % inner)


def greet(me, devices):
    barrier = pltpu.get_barrier_semaphore()

    def signal(k, carry):
        pl.semaphore_signal(
            barrier, inc=1, device_id=place((me + k) % devices),
            device_id_type=pl.DeviceIdType.MESH,
        )
        return carry

    lax.fori_loop(1, devices, signal, 0)
    return lambda: pl.semaphore_wait(barrier, devices - 1)


def ship(src, dst, send_sem, recv_sem, device):
    return pltpu.make_async_remote_copy(
        src_ref=src, dst_ref=dst, send_sem=send_sem, recv_sem=recv_sem,
        device_id=place(device), device_id_type=pl.DeviceIdType.MESH,
    )


def spread(src_ref, dst_ref, send_sems, recv_sems, me, devices):
    def start(k, carry):
        peer = (me + k) % devices
        ship(
            src_ref.at[peer], dst_ref.at[me], send_sems.at[peer], recv_sems.at[me], peer
        ).start()
        return carry

    lax.fori_loop(1, devices, start, 0)


def gather_in(src_ref, dst_ref, send_sems, recv_sems, me, devices):
    def finish(k, carry):
        peer = (me + k) % devices
        ship(
            src_ref.at[peer], dst_ref.at[peer], send_sems.at[peer], recv_sems.at[peer], peer
        ).wait()
        return carry

    lax.fori_loop(1, devices, finish, 0)


def encode_kernel(
    devices, capacity, margin,
    z_ref, coarse_ref, fine_ref, parent_ref, nbr_ref,
    w_parent_ref, w_skip_ref, taps_ref, w_cpe_ref,
    x_ref, pos_ref, got_ref, recv_ref,
    slot_ref, take_ref, par_ref, edge_ref, edge_parent_ref, skip_ref, feat_ref, send_ref,
    send_sems, recv_sems, feat_send_sems, feat_recv_sems, send_side, recv_side,
):
    me = lax.axis_index(AXES)
    entered = greet(me, devices)
    rows = z_ref.shape[1]
    coarse_rows = coarse_ref.shape[0]
    coarse = par_ref.shape[0]
    block = 256
    par_ref[margin : margin + coarse_rows, :] = jax.nn.gelu(
        layer_norm(dot(coarse_ref[...], w_parent_ref[...]))
    ).astype(BF)

    z = z_ref[...]
    dest = z // rows
    slot = z % rows
    onehot = pick(dest, devices, rows, 0)
    earlier = lax.broadcasted_iota(I32, (rows, rows), 0) < lax.broadcasted_iota(I32, (rows, rows), 1)
    ahead = dot(onehot, jnp.where(earlier, 1.0, 0.0).astype(BF))
    rank = jnp.sum(ahead * onehot.astype(F32), axis=0, keepdims=True).astype(I32)
    pos = dest * capacity + rank
    pos_ref[...] = pos

    entered()
    after, before = (me + 1) % devices, (me + devices - 1) % devices
    moves = [
        ship(
            par_ref.at[pl.ds(coarse_rows, margin), :], par_ref.at[pl.ds(0, margin), :],
            send_side.at[0], recv_side.at[0], after,
        ),
        ship(
            par_ref.at[pl.ds(margin, margin), :],
            par_ref.at[pl.ds(margin + coarse_rows, margin), :],
            send_side.at[1], recv_side.at[1], before,
        ),
        ship(
            parent_ref.at[:, pl.ds(rows - REACH, REACH)], edge_parent_ref.at[0],
            send_side.at[2], recv_side.at[2], after,
        ),
        ship(
            parent_ref.at[:, pl.ds(0, REACH)], edge_parent_ref.at[1],
            send_side.at[3], recv_side.at[3], before,
        ),
        ship(
            fine_ref.at[pl.ds(rows - REACH, REACH), :], edge_ref.at[0],
            send_side.at[4], recv_side.at[4], after,
        ),
        ship(
            fine_ref.at[pl.ds(0, REACH), :], edge_ref.at[1],
            send_side.at[5], recv_side.at[5], before,
        ),
    ]
    for move in moves:
        move.start()

    code = slot + 1
    part = lax.broadcasted_iota(I32, (16, rows), 0)
    digits = jnp.where(part == 0, code // 32, jnp.where(part == 1, code % 32, 0))
    digits = digits.astype(F32).astype(BF)
    total = devices * capacity
    step = min(512, total)
    for start in range(0, total, step):
        got = dot_nt(digits, pick(pos - start, step, rows, 0)).astype(I32)
        got = got[0:1] * 32 + got[1:2] - 1
        for d in range(step // capacity):
            slot_ref[start // capacity + d] = got[:, d * capacity : (d + 1) * capacity]
    spread(slot_ref, take_ref, send_sems, recv_sems, me, devices)
    take_ref[me] = slot_ref[me]

    def skips(i, carry):
        at = pl.ds(pl.multiple_of(i * block, block), block)
        skip_ref[at, :] = jax.nn.gelu(layer_norm(dot(fine_ref[at, :], w_skip_ref[...])))
        return carry

    lax.fori_loop(0, rows // block, skips, 0)
    base_row = me * coarse_rows - margin
    for move in moves:
        move.wait()

    for side, start in ((0, 0), (1, REACH + rows)):
        chosen = dot(
            pick(column(edge_parent_ref[side] - base_row), REACH, coarse, 1), par_ref[...]
        )
        skip = jax.nn.gelu(layer_norm(dot(edge_ref[side], w_skip_ref[...])))
        feat_ref[start : start + REACH, :] = (chosen + skip).astype(BF)

    def join(i, carry):
        base = pl.multiple_of(i * block, block)
        at = pl.ds(base, block)
        chosen = dot(pick(column(parent_ref[:, at] - base_row), block, coarse, 1), par_ref[...])
        feat_ref[pl.ds(base + REACH, block), :] = (chosen + skip_ref[at, :]).astype(BF)
        return carry

    lax.fori_loop(0, rows // block, join, 0)
    window = block + 2 * REACH

    def conv(i, carry):
        base = pl.multiple_of(i * block, block)
        at = pl.ds(base, block)
        cells = feat_ref[pl.ds(base, window), :]
        offsets = nbr_ref[:, at].T
        here = lax.broadcasted_iota(I32, offsets.shape, 0) + REACH
        source = jnp.where(offsets != REACH + 1, here + offsets, -1)
        acc = jnp.zeros((block, cells.shape[1]), F32)
        for t in range(nbr_ref.shape[0]):
            acc = acc + dot(pick(source[:, t : t + 1], block, window, 1), cells) * taps_ref[t : t + 1, :]
        out = layer_norm(dot(acc.astype(BF), w_cpe_ref[...]))
        center = feat_ref[pl.ds(base + REACH, block), :]
        x_ref[at, :] = (center.astype(F32) + out).astype(BF)
        return carry

    lax.fori_loop(0, rows // block, conv, 0)
    pos = pos_ref[...]
    per = block // capacity

    def pack(i, carry):
        sent = dot(pick(pos - i * block, block, rows, 0), x_ref[...]).astype(BF)
        send_ref[pl.ds(i * per, per)] = sent.reshape(per, capacity, sent.shape[1])
        return carry

    lax.fori_loop(0, devices // per, pack, 0)
    spread(send_ref, recv_ref, feat_send_sems, feat_recv_sems, me, devices)
    recv_ref[me] = send_ref[me]
    gather_in(slot_ref, take_ref, send_sems, recv_sems, me, devices)
    for d in range(devices):
        got_ref[:, d * capacity : (d + 1) * capacity] = take_ref[d]
    gather_in(send_ref, recv_ref, feat_send_sems, feat_recv_sems, me, devices)


def decode_kernel(
    devices, capacity, query_block,
    recv_ref, slot_row_ref, seg_ref, x_ref, pos_ref,
    w_qkv_ref, w_out_ref, w_up_ref, w_down_ref, w_cls_ref,
    out_ref,
    q_ref, k_ref, v_ref, fq_ref, fk_ref, acc_ref, home_ref, back_ref, ret_ref,
    send_sems, recv_sems,
):
    me = lax.axis_index(AXES)
    entered = greet(me, devices)
    rows, width = q_ref.shape
    total = recv_ref.shape[0]
    head_dim = width // HEADS
    lanes = 128
    per_group = lanes // head_dim
    block = 256

    def unpack(i, carry):
        at = pl.ds(pl.multiple_of(i * block, block), block)
        z = dot(pick(slot_row_ref[...] - i * block, block, total, 0), recv_ref[...])
        normed = layer_norm(z).astype(BF)
        qkv = dot(normed, w_qkv_ref[...])
        q_ref[at, :] = qkv[:, :width].astype(BF) * jnp.asarray(head_dim**-0.5, BF)
        k_ref[at, :] = qkv[:, width : 2 * width].astype(BF)
        v_ref[at, :] = qkv[:, 2 * width :].astype(BF)
        return carry

    lax.fori_loop(0, rows // block, unpack, 0)
    bits = (PATCH - 1).bit_length()
    lane = lax.broadcasted_iota(I32, (rows, lanes), 1)
    seg = jnp.broadcast_to(seg_ref[...] - seg_ref[:, 0:1], (lanes, rows)).T
    code = ((seg >> (lane // 2)) & 1) ^ (lane & 1)
    used = lane < 2 * bits
    fq_ref[...] = jnp.where(used & (code == 1), 1.0, 0.0).astype(BF)
    fk_ref[...] = jnp.where(used & (code == 0), -1e30, 0.0).astype(BF)
    owner = lane // head_dim
    per = block // capacity
    groups = width // lanes

    for g in range(groups):
        cols = slice(g * lanes, (g + 1) * lanes)
        acc_ref[...] = jnp.zeros_like(acc_ref)

        def head(h, carry):
            mine = owner == h
            keys = jnp.where(mine, k_ref[:, cols], jnp.zeros((), BF))
            keys = jnp.concatenate([keys, fk_ref[...]], axis=1)
            values = jnp.where(mine, v_ref[:, cols], jnp.zeros((), BF))
            values = jnp.concatenate([values, jnp.ones((rows, lanes), BF)], axis=1)
            for start in range(0, rows, query_block):
                at = slice(start, start + query_block)
                query = jnp.concatenate([q_ref[at, cols], fq_ref[at, :]], axis=1)
                scores = dot_nt(query, keys)
                top = jnp.max(scores, axis=-1, keepdims=True)
                probs = jnp.exp(scores - top).astype(BF)
                out = dot(probs, values)
                acc_ref[at, :] += out[:, :lanes] / out[:, lanes:]
            return carry

        lax.fori_loop(0, per_group, head, 0)
        home_ref[:, cols] = acc_ref[...].astype(BF)

        def pack(i, carry):
            at = pl.ds(pl.multiple_of(i * block, block), block)
            sent = dot(pick(column(slot_row_ref[:, at]), block, rows, 1), home_ref[:, cols])
            back_ref[g, pl.ds(i * per, per)] = sent.astype(BF).reshape(per, capacity, lanes)
            return carry

        lax.fori_loop(0, devices // per, pack, 0)
        if g == 0:
            entered()
        spread(back_ref.at[g], ret_ref.at[g], send_sems.at[g], recv_sems.at[g], me, devices)
        ret_ref[g, me] = back_ref[g, me]

    for g in range(groups):
        cols = slice(g * lanes, (g + 1) * lanes)
        gather_in(back_ref.at[g], ret_ref.at[g], send_sems.at[g], recv_sems.at[g], me, devices)
        returned = ret_ref[g].reshape(total, lanes)
        for start in range(0, rows, block):
            at = slice(start, start + block)
            home = dot(pick(column(pos_ref[:, at]), block, total, 1), returned)
            home_ref[at, cols] = home.astype(BF)

    for start in range(0, rows, block):
        at = slice(start, start + block)
        o = dot(home_ref[at, :], w_out_ref[...]).astype(BF)
        x_two = x_ref[at, :].astype(F32) + o.astype(F32)
        hidden = jax.nn.gelu(dot(layer_norm(x_two).astype(BF), w_up_ref[...])).astype(BF)
        x_three = x_two + dot(hidden, w_down_ref[...])
        out_ref[:, at] = dot_nt(w_cls_ref[...], layer_norm(x_three).astype(BF))


def local(
    coarse_feats,
    fine_feats,
    parent_index,
    nbr_offset,
    z_position,
    segment_id,
    w_parent,
    w_skip,
    conv_taps,
    w_cpe,
    w_qkv,
    w_out,
    w_up,
    w_down,
    w_cls,
):
    fine_rows, width = fine_feats.shape
    coarse_rows = coarse_feats.shape[0]
    devices = lax.axis_size(AXES)
    capacity = 2 * fine_rows // devices
    total = devices * capacity
    assert fine_rows == PATCH

    fine_per_coarse = fine_rows // coarse_rows
    margin = coarse_rows // 2 + REACH // fine_per_coarse
    lanes = 128
    groups = width // lanes
    pair = pltpu.SemaphoreType.DMA((devices,))
    x_feats, pos, slots, recv = pl.pallas_call(
        functools.partial(encode_kernel, devices, capacity, margin),
        out_shape=(
            jax.ShapeDtypeStruct((fine_rows, width), BF),
            jax.ShapeDtypeStruct((1, fine_rows), I32),
            jax.ShapeDtypeStruct((1, total), I32),
            jax.ShapeDtypeStruct((devices, capacity, width), BF),
        ),
        in_specs=[VM] * 9,
        out_specs=(VM,) * 4,
        scratch_shapes=[
            pltpu.VMEM((devices, 1, capacity), I32),
            pltpu.VMEM((devices, 1, capacity), I32),
            pltpu.VMEM((coarse_rows + 2 * margin, width), BF),
            pltpu.VMEM((2, REACH, width), BF),
            pltpu.VMEM((2, 1, REACH), I32),
            pltpu.VMEM((fine_rows, width), F32),
            pltpu.VMEM((fine_rows + 2 * REACH, width), BF),
            pltpu.VMEM((devices, capacity, width), BF),
            pair, pair, pair, pair,
            pltpu.SemaphoreType.DMA((6,)),
            pltpu.SemaphoreType.DMA((6,)),
        ],
        compiler_params=pltpu.CompilerParams(collective_id=0, has_side_effects=True),
    )(
        z_position.reshape(1, fine_rows), coarse_feats, fine_feats,
        parent_index.reshape(1, fine_rows), nbr_offset,
        w_parent, w_skip, conv_taps, w_cpe,
    )
    return pl.pallas_call(
        functools.partial(decode_kernel, devices, capacity, QUERY_BLOCK),
        out_shape=jax.ShapeDtypeStruct((w_cls.shape[0], fine_rows), F32),
        in_specs=[VM] * 10,
        out_specs=VM,
        scratch_shapes=[
            pltpu.VMEM((fine_rows, width), BF),
            pltpu.VMEM((fine_rows, width), BF),
            pltpu.VMEM((fine_rows, width), BF),
            pltpu.VMEM((fine_rows, lanes), BF),
            pltpu.VMEM((fine_rows, lanes), BF),
            pltpu.VMEM((fine_rows, lanes), F32),
            pltpu.VMEM((fine_rows, width), BF),
            pltpu.VMEM((groups, devices, capacity, lanes), BF),
            pltpu.VMEM((groups, devices, capacity, lanes), BF),
            pltpu.SemaphoreType.DMA((groups, devices)),
            pltpu.SemaphoreType.DMA((groups, devices)),
        ],
        compiler_params=pltpu.CompilerParams(collective_id=1, has_side_effects=True),
    )(
        recv.reshape(total, width), slots, segment_id.reshape(1, fine_rows), x_feats, pos,
        w_qkv, w_out, w_up, w_down, w_cls,
    )


def solution(mesh):
    rows = P(AXES, None)
    flat = P(AXES)
    placed = (rows, rows, flat, P(None, AXES), flat, flat) + (P(),) * 9
    return jax.shard_map(
        local, mesh=mesh, in_specs=placed, out_specs=P(None, AXES), check_vma=False
    )
```

```python
import functools

import jax
import jax.numpy as jnp
from jax import lax
from jax.experimental import pallas as pl
from jax.experimental.pallas import tpu as pltpu
from jax.sharding import PartitionSpec as P

HEADS = 16
PATCH = 1024
REACH = 256
QUERY_BLOCK = 512
AXES = ("row", "col")
BF = jnp.bfloat16
F32 = jnp.float32
I32 = jnp.int32
VM = pl.BlockSpec(memory_space=pltpu.VMEM)


def dot(a, b):
    return jnp.dot(a, b, preferred_element_type=F32)


def dot_nt(a, b):
    return lax.dot_general(a, b, (((1,), (1,)), ((), ())), preferred_element_type=F32)


def layer_norm(values):
    center = values - jnp.mean(values, axis=-1, keepdims=True)
    spread = jnp.mean(center * center, axis=-1, keepdims=True)
    return center * lax.rsqrt(spread + 1e-05)


def pick(index, rows, cols, dim):
    shape = (rows, cols)
    grid = lax.broadcasted_iota(I32, shape, dim).astype(jnp.int16)
    want = jnp.broadcast_to(jnp.clip(index, -1, 32767), shape).astype(jnp.int16)
    return jnp.where(grid == want, jnp.ones((), BF), jnp.zeros((), BF))


def column(row):
    return jnp.broadcast_to(row, (128, row.shape[1])).T[:, :1]


def place(device):
    inner = lax.axis_size("col")
    return (device // inner, device % inner)


def greet(me, devices):
    barrier = pltpu.get_barrier_semaphore()

    def signal(k, carry):
        pl.semaphore_signal(
            barrier, inc=1, device_id=place((me + k) % devices),
            device_id_type=pl.DeviceIdType.MESH,
        )
        return carry

    lax.fori_loop(1, devices, signal, 0)
    return lambda: pl.semaphore_wait(barrier, devices - 1)


def ship(src, dst, send_sem, recv_sem, device):
    return pltpu.make_async_remote_copy(
        src_ref=src, dst_ref=dst, send_sem=send_sem, recv_sem=recv_sem,
        device_id=place(device), device_id_type=pl.DeviceIdType.MESH,
    )


def spread(src_ref, dst_ref, send_sems, recv_sems, me, devices):
    def start(k, carry):
        peer = (me + k) % devices
        ship(
            src_ref.at[peer], dst_ref.at[me], send_sems.at[peer], recv_sems.at[me], peer
        ).start()
        return carry

    lax.fori_loop(1, devices, start, 0)


def gather_in(src_ref, dst_ref, send_sems, recv_sems, me, devices):
    def finish(k, carry):
        peer = (me + k) % devices
        ship(
            src_ref.at[peer], dst_ref.at[peer], send_sems.at[peer], recv_sems.at[peer], peer
        ).wait()
        return carry

    lax.fori_loop(1, devices, finish, 0)


def encode_kernel(
    devices, capacity, margin,
    z_ref, coarse_ref, fine_ref, parent_ref, nbr_ref,
    w_parent_ref, w_skip_ref, taps_ref, w_cpe_ref,
    x_ref, pos_ref, got_ref, recv_ref,
    slot_ref, take_ref, par_ref, edge_ref, edge_parent_ref, skip_ref, feat_ref, send_ref,
    send_sems, recv_sems, feat_send_sems, feat_recv_sems, send_side, recv_side,
):
    me = lax.axis_index(AXES)
    entered = greet(me, devices)
    rows = z_ref.shape[1]
    coarse_rows = coarse_ref.shape[0]
    coarse = par_ref.shape[0]
    block = 256
    par_ref[margin : margin + coarse_rows, :] = jax.nn.gelu(
        layer_norm(dot(coarse_ref[...], w_parent_ref[...]))
    ).astype(BF)

    z = z_ref[...]
    dest = z // rows
    slot = z % rows
    onehot = pick(dest, devices, rows, 0)
    earlier = lax.broadcasted_iota(I32, (rows, rows), 0) < lax.broadcasted_iota(I32, (rows, rows), 1)
    ahead = dot(onehot, jnp.where(earlier, 1.0, 0.0).astype(BF))
    rank = jnp.sum(ahead * onehot.astype(F32), axis=0, keepdims=True).astype(I32)
    pos = dest * capacity + rank
    pos_ref[...] = pos

    entered()
    after, before = (me + 1) % devices, (me + devices - 1) % devices
    moves = [
        ship(
            par_ref.at[pl.ds(coarse_rows, margin), :], par_ref.at[pl.ds(0, margin), :],
            send_side.at[0], recv_side.at[0], after,
        ),
        ship(
            par_ref.at[pl.ds(margin, margin), :],
            par_ref.at[pl.ds(margin + coarse_rows, margin), :],
            send_side.at[1], recv_side.at[1], before,
        ),
        ship(
            parent_ref.at[:, pl.ds(rows - REACH, REACH)], edge_parent_ref.at[0],
            send_side.at[2], recv_side.at[2], after,
        ),
        ship(
            parent_ref.at[:, pl.ds(0, REACH)], edge_parent_ref.at[1],
            send_side.at[3], recv_side.at[3], before,
        ),
        ship(
            fine_ref.at[pl.ds(rows - REACH, REACH), :], edge_ref.at[0],
            send_side.at[4], recv_side.at[4], after,
        ),
        ship(
            fine_ref.at[pl.ds(0, REACH), :], edge_ref.at[1],
            send_side.at[5], recv_side.at[5], before,
        ),
    ]
    for move in moves:
        move.start()

    code = slot + 1
    part = lax.broadcasted_iota(I32, (16, rows), 0)
    digits = jnp.where(part == 0, code // 32, jnp.where(part == 1, code % 32, 0))
    digits = digits.astype(F32).astype(BF)
    total = devices * capacity
    step = min(512, total)
    for start in range(0, total, step):
        got = dot_nt(digits, pick(pos - start, step, rows, 0)).astype(I32)
        got = got[0:1] * 32 + got[1:2] - 1
        for d in range(step // capacity):
            slot_ref[start // capacity + d] = got[:, d * capacity : (d + 1) * capacity]
    spread(slot_ref, take_ref, send_sems, recv_sems, me, devices)
    take_ref[me] = slot_ref[me]

    def skips(i, carry):
        at = pl.ds(pl.multiple_of(i * block, block), block)
        skip_ref[at, :] = jax.nn.gelu(layer_norm(dot(fine_ref[at, :], w_skip_ref[...])))
        return carry

    lax.fori_loop(0, rows // block, skips, 0)
    base_row = me * coarse_rows - margin
    for move in moves:
        move.wait()

    for side, start in ((0, 0), (1, REACH + rows)):
        chosen = dot(
            pick(column(edge_parent_ref[side] - base_row), REACH, coarse, 1), par_ref[...]
        )
        skip = jax.nn.gelu(layer_norm(dot(edge_ref[side], w_skip_ref[...])))
        feat_ref[start : start + REACH, :] = (chosen + skip).astype(BF)

    def join(i, carry):
        base = pl.multiple_of(i * block, block)
        at = pl.ds(base, block)
        chosen = dot(pick(column(parent_ref[:, at] - base_row), block, coarse, 1), par_ref[...])
        feat_ref[pl.ds(base + REACH, block), :] = (chosen + skip_ref[at, :]).astype(BF)
        return carry

    lax.fori_loop(0, rows // block, join, 0)
    window = block + 2 * REACH

    def conv(i, carry):
        base = pl.multiple_of(i * block, block)
        at = pl.ds(base, block)
        cells = feat_ref[pl.ds(base, window), :]
        offsets = nbr_ref[:, at].T
        here = lax.broadcasted_iota(I32, offsets.shape, 0) + REACH
        source = jnp.where(offsets != REACH + 1, here + offsets, -1)
        acc = jnp.zeros((block, cells.shape[1]), F32)
        for t in range(nbr_ref.shape[0]):
            acc = acc + dot(pick(source[:, t : t + 1], block, window, 1), cells) * taps_ref[t : t + 1, :]
        out = layer_norm(dot(acc.astype(BF), w_cpe_ref[...]))
        center = feat_ref[pl.ds(base + REACH, block), :]
        x_ref[at, :] = (center.astype(F32) + out).astype(BF)
        return carry

    lax.fori_loop(0, rows // block, conv, 0)
    pos = pos_ref[...]
    per = block // capacity

    def pack(i, carry):
        sent = dot(pick(pos - i * block, block, rows, 0), x_ref[...]).astype(BF)
        send_ref[pl.ds(i * per, per)] = sent.reshape(per, capacity, sent.shape[1])
        return carry

    lax.fori_loop(0, devices // per, pack, 0)
    spread(send_ref, recv_ref, feat_send_sems, feat_recv_sems, me, devices)
    recv_ref[me] = send_ref[me]
    gather_in(slot_ref, take_ref, send_sems, recv_sems, me, devices)
    for d in range(devices):
        got_ref[:, d * capacity : (d + 1) * capacity] = take_ref[d]
    gather_in(send_ref, recv_ref, feat_send_sems, feat_recv_sems, me, devices)


def decode_kernel(
    devices, capacity, query_block,
    recv_ref, slot_row_ref, seg_ref, x_ref, pos_ref,
    w_qkv_ref, w_out_ref, w_up_ref, w_down_ref, w_cls_ref,
    out_ref,
    q_ref, k_ref, v_ref, fq_ref, fk_ref, acc_ref, home_ref, back_ref, ret_ref,
    send_sems, recv_sems,
):
    me = lax.axis_index(AXES)
    entered = greet(me, devices)
    rows, width = q_ref.shape
    total = recv_ref.shape[0]
    head_dim = width // HEADS
    lanes = 128
    per_group = lanes // head_dim
    block = 256

    def unpack(i, carry):
        at = pl.ds(pl.multiple_of(i * block, block), block)
        z = dot(pick(slot_row_ref[...] - i * block, block, total, 0), recv_ref[...])
        normed = layer_norm(z).astype(BF)
        qkv = dot(normed, w_qkv_ref[...])
        q_ref[at, :] = qkv[:, :width].astype(BF) * jnp.asarray(head_dim**-0.5, BF)
        k_ref[at, :] = qkv[:, width : 2 * width].astype(BF)
        v_ref[at, :] = qkv[:, 2 * width :].astype(BF)
        return carry

    lax.fori_loop(0, rows // block, unpack, 0)
    bits = (PATCH - 1).bit_length()
    lane = lax.broadcasted_iota(I32, (rows, lanes), 1)
    seg = jnp.broadcast_to(seg_ref[...] - seg_ref[:, 0:1], (lanes, rows)).T
    code = ((seg >> (lane // 2)) & 1) ^ (lane & 1)
    used = lane < 2 * bits
    fq_ref[...] = jnp.where(used & (code == 1), 1.0, 0.0).astype(BF)
    fk_ref[...] = jnp.where(used & (code == 0), -1e30, 0.0).astype(BF)
    owner = lane // head_dim
    per = block // capacity
    groups = width // lanes

    for g in range(groups):
        cols = slice(g * lanes, (g + 1) * lanes)
        acc_ref[...] = jnp.zeros_like(acc_ref)

        def head(h, carry):
            mine = owner == h
            keys = jnp.where(mine, k_ref[:, cols], jnp.zeros((), BF))
            keys = jnp.concatenate([keys, fk_ref[...]], axis=1)
            values = jnp.where(mine, v_ref[:, cols], jnp.zeros((), BF))
            values = jnp.concatenate([values, jnp.ones((rows, lanes), BF)], axis=1)
            for start in range(0, rows, query_block):
                at = slice(start, start + query_block)
                query = jnp.concatenate([q_ref[at, cols], fq_ref[at, :]], axis=1)
                scores = dot_nt(query, keys)
                top = jnp.max(scores, axis=-1, keepdims=True)
                probs = jnp.exp(scores - top).astype(BF)
                out = dot(probs, values)
                acc_ref[at, :] += out[:, :lanes] / out[:, lanes:]
            return carry

        lax.fori_loop(0, per_group, head, 0)
        home_ref[:, cols] = acc_ref[...].astype(BF)

        def pack(i, carry):
            at = pl.ds(pl.multiple_of(i * block, block), block)
            sent = dot(pick(column(slot_row_ref[:, at]), block, rows, 1), home_ref[:, cols])
            back_ref[g, pl.ds(i * per, per)] = sent.astype(BF).reshape(per, capacity, lanes)
            return carry

        lax.fori_loop(0, devices // per, pack, 0)
        if g == 0:
            entered()
        spread(back_ref.at[g], ret_ref.at[g], send_sems.at[g], recv_sems.at[g], me, devices)
        ret_ref[g, me] = back_ref[g, me]

    for g in range(groups):
        cols = slice(g * lanes, (g + 1) * lanes)
        gather_in(back_ref.at[g], ret_ref.at[g], send_sems.at[g], recv_sems.at[g], me, devices)
        returned = ret_ref[g].reshape(total, lanes)
        for start in range(0, rows, block):
            at = slice(start, start + block)
            home = dot(pick(column(pos_ref[:, at]), block, total, 1), returned)
            home_ref[at, cols] = home.astype(BF)

    for start in range(0, rows, block):
        at = slice(start, start + block)
        o = dot(home_ref[at, :], w_out_ref[...]).astype(BF)
        x_two = x_ref[at, :].astype(F32) + o.astype(F32)
        hidden = jax.nn.gelu(dot(layer_norm(x_two).astype(BF), w_up_ref[...])).astype(BF)
        x_three = x_two + dot(hidden, w_down_ref[...])
        out_ref[:, at] = dot_nt(w_cls_ref[...], layer_norm(x_three).astype(BF))


def local(
    coarse_feats,
    fine_feats,
    parent_index,
    nbr_offset,
    z_position,
    segment_id,
    w_parent,
    w_skip,
    conv_taps,
    w_cpe,
    w_qkv,
    w_out,
    w_up,
    w_down,
    w_cls,
):
    fine_rows, width = fine_feats.shape
    coarse_rows = coarse_feats.shape[0]
    devices = lax.axis_size(AXES)
    capacity = 2 * fine_rows // devices
    total = devices * capacity
    assert fine_rows == PATCH

    fine_per_coarse = fine_rows // coarse_rows
    margin = coarse_rows // 2 + REACH // fine_per_coarse
    lanes = 128
    groups = width // lanes
    pair = pltpu.SemaphoreType.DMA((devices,))
    x_feats, pos, slots, recv = pl.pallas_call(
        functools.partial(encode_kernel, devices, capacity, margin),
        out_shape=(
            jax.ShapeDtypeStruct((fine_rows, width), BF),
            jax.ShapeDtypeStruct((1, fine_rows), I32),
            jax.ShapeDtypeStruct((1, total), I32),
            jax.ShapeDtypeStruct((devices, capacity, width), BF),
        ),
        in_specs=[VM] * 9,
        out_specs=(VM,) * 4,
        scratch_shapes=[
            pltpu.VMEM((devices, 1, capacity), I32),
            pltpu.VMEM((devices, 1, capacity), I32),
            pltpu.VMEM((coarse_rows + 2 * margin, width), BF),
            pltpu.VMEM((2, REACH, width), BF),
            pltpu.VMEM((2, 1, REACH), I32),
            pltpu.VMEM((fine_rows, width), F32),
            pltpu.VMEM((fine_rows + 2 * REACH, width), BF),
            pltpu.VMEM((devices, capacity, width), BF),
            pair, pair, pair, pair,
            pltpu.SemaphoreType.DMA((6,)),
            pltpu.SemaphoreType.DMA((6,)),
        ],
        compiler_params=pltpu.CompilerParams(collective_id=0, has_side_effects=True),
    )(
        z_position.reshape(1, fine_rows), coarse_feats, fine_feats,
        parent_index.reshape(1, fine_rows), nbr_offset,
        w_parent, w_skip, conv_taps, w_cpe,
    )
    return pl.pallas_call(
        functools.partial(decode_kernel, devices, capacity, QUERY_BLOCK),
        out_shape=jax.ShapeDtypeStruct((w_cls.shape[0], fine_rows), F32),
        in_specs=[VM] * 10,
        out_specs=VM,
        scratch_shapes=[
            pltpu.VMEM((fine_rows, width), BF),
            pltpu.VMEM((fine_rows, width), BF),
            pltpu.VMEM((fine_rows, width), BF),
            pltpu.VMEM((fine_rows, lanes), BF),
            pltpu.VMEM((fine_rows, lanes), BF),
            pltpu.VMEM((fine_rows, lanes), F32),
            pltpu.VMEM((fine_rows, width), BF),
            pltpu.VMEM((groups, devices, capacity, lanes), BF),
            pltpu.VMEM((groups, devices, capacity, lanes), BF),
            pltpu.SemaphoreType.DMA((groups, devices)),
            pltpu.SemaphoreType.DMA((groups, devices)),
        ],
        compiler_params=pltpu.CompilerParams(collective_id=1, has_side_effects=True),
    )(
        recv.reshape(total, width), slots, segment_id.reshape(1, fine_rows), x_feats, pos,
        w_qkv, w_out, w_up, w_down, w_cls,
    )


def solution(mesh):
    rows = P(AXES, None)
    flat = P(AXES)
    placed = (rows, rows, flat, P(None, AXES), flat, flat) + (P(),) * 9
    return jax.shard_map(
        local, mesh=mesh, in_specs=placed, out_specs=P(None, AXES), check_vma=False
    )
```
